512 devices in a mesh: coil: 16 (over x, z_hi, core), slab: 32 (over y, z_lo).
Axes of the slice: x: 4, y: 4, z: 16 (z_hi: 2, z_lo: 8; z = z_hi * 8 + z_lo), core: 2. Of those that a mesh axis runs over, the one named last changes fastest.
Arguments:
- kspace: bfloat16 [2, 32, 2, 32, 384, 128], P(None, 'coil', None, None, 'slab'), may hold values from -6 to 6
- coil_maps: bfloat16 [2, 32, 32, 384, 384], P(None, 'coil', None, 'slab'), may hold values from -1.1953125 to 1.1953125
- line_index: int32 [2, 384, 128], P(None, 'slab'), may hold values from 0 to 383, as said below
Outputs:
- harmonic_image: float32 [32, 2, 384, 384], P('coil', None, 'slab')
The draws below stay inside these ranges and needn't reach their ends.
Inputs may be any that keep to these rules, and one draw needn't show every extreme that they name: `line_index`: for each phase offset and kz plane the 128 ky indices are distinct.
All inputs are finite; a program needn't handle non-finite values.
Results may differ from the reference program's by a relative error of at most 0.0043.
Values may be sent and summed in bfloat16 or wider, within the bound.
No kernel may reach another device: no remote copies, remote signals or barrier semaphores. Data moves between devices by JAX's collectives and lax.ppermute only.
A program may use at most 64 MiB of HBM per device.

```python
import math
import jax
import jax.numpy as jnp
from jax import lax

NY = 384
NZ = 384
LINES = 128
OFFS = 2
PHASES = 8
XR = 32
COILS = 32


def pick_row(row_key):
    return jax.random.permutation(row_key, NY)[:LINES]


def draw_line_index(key, part):
    row_keys = jax.random.split(jax.random.fold_in(key, 17), OFFS * NZ)
    chosen = jax.vmap(pick_row)(row_keys)
    return chosen.reshape(OFFS, NZ, LINES).astype(jnp.int32)


def raised(result, rng, source, target, shards_of, factor):
    def block_of(position):
        return (jnp.arange(result.shape[position]) // (result.shape[position] // shards_of)).reshape((-1,) + (1,) * (result.ndim - 1 - position))

    first = jax.random.permutation(rng, shards_of)[block_of(target)]
    second = (block_of(target) + shards_of // 2) % shards_of
    return jnp.where((block_of(source) == first) | (block_of(source) == second), factor * result, result)


def level_of(key, dims, shards, least, top_value):
    level = 1.0
    for axis_at, parts in shards:
        draws = jax.random.uniform(jax.random.fold_in(jax.random.fold_in(key, 6), axis_at), (parts,), jnp.float32, least / len(shards), top_value / len(shards))
        level = level * jnp.repeat(jnp.exp(draws), dims[axis_at] // parts).reshape((-1,) + (1,) * (len(dims) - 1 - axis_at))
    return level


def bell_draw(own_key, dims, scale, most, pieces=(), kind=jnp.bfloat16):
    array = scale * jax.random.normal(own_key, dims, jnp.float32)
    if pieces:
        array = array * level_of(own_key, dims, pieces, -0.22, 0.18)
    return jnp.clip(array, -most, most).astype(kind)


def heavy_noise(rng, shape, width, limit, pieces, heavy, dtype=jnp.bfloat16):
    values = width * jax.random.normal(rng, shape, jnp.float32)
    if pieces:
        values = values * level_of(rng, shape, pieces, -0.22, 0.18)
    return jnp.clip(raised(values, jax.random.fold_in(rng, 3), *heavy), -limit, limit).astype(dtype)


def setup_inputs(seed: int = 0) -> dict:
    arg_keys = jax.random.split(jax.random.key(seed), 4)
    return {
        "kspace": bell_draw(arg_keys[0], (2, COILS, OFFS, XR, NZ, LINES), 1.0, 6.0, ((1, 16), (4, 32))),
        "coil_maps": heavy_noise(arg_keys[1], (2, COILS, XR, NY, NZ), 0.2, 1.1953125, ((1, 16), (3, 32)), (1, 2, 16, 2.0)),
        "line_index": draw_line_index(jax.random.fold_in(arg_keys[3], 71), 0),
    }


def line_tables(line_index, length):
    positions = lax.broadcasted_iota(jnp.int32, (1, 1, 1, length), 3)
    turn_count = line_index[..., None] * positions % length
    angles = turn_count.astype(jnp.float32) * (2.0 * math.pi / length)
    scaling = 1.0 / math.sqrt(length)
    return ((jnp.cos(angles) * scaling).astype(jnp.bfloat16), (jnp.sin(angles) * scaling).astype(jnp.bfloat16))

def dense_tables(length):
    row_pos = lax.broadcasted_iota(jnp.int32, (length, length), 0)
    col_pos = lax.broadcasted_iota(jnp.int32, (length, length), 1)
    turn_count = row_pos * col_pos % length
    angles = turn_count.astype(jnp.float32) * (2.0 * math.pi / length)
    scaling = 1.0 / math.sqrt(length)
    return ((jnp.cos(angles) * scaling).astype(jnp.bfloat16), (jnp.sin(angles) * scaling).astype(jnp.bfloat16))

def fold_offsets(real_part, imag_part, fold_axis):
    sum_real = None
    sum_imag = None
    for offset in range(real_part.shape[fold_axis]):
        phase_angle = 2.0 * math.pi * offset / PHASES
        cosine = math.cos(phase_angle)
        sine = math.sin(phase_angle)
        here_real = jnp.take(real_part, offset, axis=fold_axis)
        here_imag = jnp.take(imag_part, offset, axis=fold_axis)
        term_real = cosine * here_real + sine * here_imag
        term_imag = cosine * here_imag - sine * here_real
        if sum_real is None:
            sum_real, sum_imag = (term_real, term_imag)
        else:
            sum_real, sum_imag = (sum_real + term_real, sum_imag + term_imag)
    return jnp.stack([sum_real, sum_imag]).astype(jnp.bfloat16)

def reference(kspace, coil_maps, line_index):
    line_cos, line_sin = line_tables(line_index, NY)
    line_cos = line_cos.astype(jnp.float32)
    line_sin = line_sin.astype(jnp.float32)
    depth_cos, depth_sin = dense_tables(NZ)
    depth_cos = depth_cos.astype(jnp.float32)
    depth_sin = depth_sin.astype(jnp.float32)
    highest = lax.Precision.HIGHEST

    def one_coil(coil, totals):
        samples = lax.dynamic_index_in_dim(kspace, coil, 1, keepdims=False).astype(jnp.float32)

        def lines_to_rows(left, right):
            return jnp.einsum('txkl,tkly->txyk', left, right, precision=highest)
        hybrid_real = lines_to_rows(samples[0], line_cos) - lines_to_rows(samples[1], line_sin)
        hybrid_imag = lines_to_rows(samples[0], line_sin) + lines_to_rows(samples[1], line_cos)
        folded = fold_offsets(hybrid_real, hybrid_imag, 0).astype(jnp.float32)

        def depth(left, right):
            return jnp.einsum('xyk,kz->xyz', left, right, precision=highest)
        image_real = depth(folded[0], depth_cos) - depth(folded[1], depth_sin)
        image_imag = depth(folded[0], depth_sin) + depth(folded[1], depth_cos)
        maps = lax.dynamic_index_in_dim(coil_maps, coil, 1, keepdims=False).astype(jnp.float32)
        add_real = maps[0] * image_real + maps[1] * image_imag
        add_imag = maps[0] * image_imag - maps[1] * image_real
        return (totals[0] + add_real, totals[1] + add_imag)
    zeros = jnp.zeros((XR, NY, NZ), jnp.float32)
    sum_real, sum_imag = lax.fori_loop(0, COILS, one_coil, (zeros, zeros))
    return jnp.stack([sum_real, sum_imag], axis=1)
```

```python
import functools
import math

import jax
import jax.numpy as jnp
import numpy as np
from jax import lax
from jax.experimental import pallas as pl
from jax.experimental.pallas import tpu as pltpu
from jax.sharding import PartitionSpec as P

NY = 384
NZ = 384
PHASES = 8
SLABS = 32
YL = NY // SLABS
KZL = NZ // SLABS
PAIRS = YL // 2
XR = 32
ROWS = KZL * 2
GROUPS = SLABS * PAIRS


def dft(rows, cols, length):
    turns = np.outer(rows, cols) % length
    angles = turns * (2.0 * math.pi / length)
    scaling = 1.0 / math.sqrt(length)
    return np.cos(angles) * scaling, np.sin(angles) * scaling


@functools.cache
def row_table():
    y = np.arange(SLABS)[:, None] * YL + np.arange(PAIRS)[None, :] * 2
    y = np.stack([y.reshape(-1), y.reshape(-1) + 1]).reshape(-1)
    cosine, sine = dft(y, np.arange(NY), NY)
    return np.concatenate([cosine, sine], axis=0).astype(jnp.bfloat16)


@functools.cache
def depth_table():
    cosine, sine = dft(np.arange(NZ), np.arange(NZ), NZ)
    from_real = np.concatenate([cosine, sine], axis=1)
    from_imag = np.concatenate([-sine, cosine], axis=1)
    return np.stack([from_real, from_imag], axis=1).reshape(2 * NZ, 2 * NZ).astype(jnp.bfloat16)


def encode_kernel(k_ref, line_ref, w_ref, out_ref, scratch):
    theta = 2.0 * math.pi / PHASES
    cosine = math.cos(theta)
    sine = math.sin(theta)
    ky = lax.broadcasted_iota(jnp.int32, (NY, 128), 0)
    low = lax.broadcasted_iota(jnp.int32, (GROUPS, 128), 1) < 64

    def grid_of(kz):
        first = jnp.concatenate([k_ref[r, c, 0, kz] for r in range(2) for c in range(2)], axis=0)
        later_re = jnp.concatenate([k_ref[0, c, 1, kz] for c in range(2)], axis=0).astype(jnp.float32)
        later_im = jnp.concatenate([k_ref[1, c, 1, kz] for c in range(2)], axis=0).astype(jnp.float32)
        later = jnp.concatenate(
            [cosine * later_re + sine * later_im, cosine * later_im - sine * later_re], axis=0
        ).astype(jnp.bfloat16)
        samples = jnp.concatenate([first, later], axis=1)
        chosen = jnp.concatenate(
            [jnp.where(ky == line_ref[kz, t : t + 1, :], 1.0, 0.0).astype(jnp.bfloat16) for t in range(2)],
            axis=1,
        )
        placed = lax.dot_general(
            chosen, samples, (((1,), (1,)), ((), ())), preferred_element_type=jnp.float32
        )
        return placed.astype(jnp.bfloat16)

    def split(a, b):
        swapped = pltpu.roll(jnp.where(low, b, a), 64, 1)
        return jnp.where(low, a, swapped), jnp.where(low, swapped, b)

    for pair in range(KZL // 2):
        grids = jnp.concatenate([grid_of(2 * pair), grid_of(2 * pair + 1)], axis=1)
        both = jnp.dot(w_ref[...], grids, preferred_element_type=jnp.float32)
        for half in range(2):
            kz = 2 * pair + half
            part = both[:, half * 128 : half * 128 + 128]
            cos_re, cos_im = split(part[:GROUPS], part[GROUPS : 2 * GROUPS])
            sin_re, sin_im = split(part[2 * GROUPS : 3 * GROUPS], part[3 * GROUPS :])
            scratch[pl.ds(2 * kz, GROUPS, stride=ROWS), :] = cos_re - sin_im
            scratch[pl.ds(2 * kz + 1, GROUPS, stride=ROWS), :] = sin_re + cos_im
    out_ref[...] = scratch[...].astype(jnp.bfloat16)


def encode(kspace, line_index):
    return pl.pallas_call(
        encode_kernel,
        out_shape=jax.ShapeDtypeStruct((GROUPS * ROWS, 128), jnp.bfloat16),
        in_specs=[pl.BlockSpec(memory_space=pltpu.VMEM)] * 3,
        out_specs=pl.BlockSpec(memory_space=pltpu.VMEM),
        scratch_shapes=[pltpu.VMEM((GROUPS * ROWS, 128), jnp.float32)],
        name="encode",
    )(jnp.transpose(kspace, (0, 1, 2, 4, 3, 5)), jnp.transpose(line_index, (1, 0, 2)), jnp.asarray(row_table()))


def image_kernel(r_ref, m_ref, d_ref, out_ref, scratch):
    for pair in range(PAIRS):
        arrived = r_ref[:, pair].astype(jnp.float32).reshape(SLABS * ROWS, 128)
        lhs = arrived.T.astype(jnp.bfloat16)
        image = jnp.dot(lhs, d_ref[...], preferred_element_type=jnp.float32)
        for which in range(2):
            y = 2 * pair + which
            real = None
            for c in range(2):
                start = which * 64 + c * 32
                image_re = image[start : start + 32, :NZ]
                image_im = image[start : start + 32, NZ:]
                map_re = m_ref[0, c, y].astype(jnp.float32)
                map_im = m_ref[1, c, y].astype(jnp.float32)
                add_re = map_re * image_re + map_im * image_im
                add_im = map_re * image_im - map_im * image_re
                real, imag = (add_re, add_im) if real is None else (real + add_re, imag + add_im)
            for part, value in enumerate((real, imag)):
                for lane in range(3):
                    scratch[lane, pl.ds(2 * y + part, XR, stride=ROWS), :] = value[:, lane * 128 : lane * 128 + 128]
    block = 2 * ROWS
    for xs in range(4):
        for zh in range(2):
            for core in range(2):
                src = (xs * 4 + zh * 2 + core) * block
                dst = (xs * 4 + core * 2 + zh) * block
                for lane in range(3):
                    out_ref[dst : dst + block, lane * 128 : lane * 128 + 128] = scratch[
                        lane, src : src + block, :
                    ].astype(jnp.bfloat16)


def images(arrived, coil_maps):
    return pl.pallas_call(
        image_kernel,
        out_shape=jax.ShapeDtypeStruct((XR * ROWS, NZ), jnp.bfloat16),
        in_specs=[pl.BlockSpec(memory_space=pltpu.VMEM)] * 3,
        out_specs=pl.BlockSpec(memory_space=pltpu.VMEM),
        scratch_shapes=[pltpu.VMEM((3, XR * ROWS, 128), jnp.float32)],
        name="images",
    )(
        arrived.reshape(SLABS, PAIRS, ROWS, 128),
        jnp.transpose(coil_maps, (0, 1, 3, 2, 4)),
        jnp.asarray(depth_table()),
    )


NEAR = [[x * 4 + far * 2 + core for x in range(4) for core in range(2)] for far in range(2)]
ACROSS = [(i, i ^ 2) for i in range(16)]


def combine(partial):
    arrived = lax.all_to_all(
        partial.reshape(8, 4 * ROWS, NZ), "coil", split_axis=0, concat_axis=0, tiled=True, axis_index_groups=NEAR
    )
    near = arrived.astype(jnp.float32).sum(axis=0).reshape(2, 2 * ROWS, NZ)
    far = (lax.axis_index("coil") // 2) % 2
    own = lax.dynamic_index_in_dim(near, far, 0, keepdims=False)
    other = lax.dynamic_index_in_dim(near, 1 - far, 0, keepdims=False)
    total = own + lax.ppermute(other, "coil", ACROSS)
    return jnp.transpose(total.reshape(2, YL, 2, NZ), (0, 2, 1, 3))


def local(kspace, coil_maps, line_index):
    sent = encode(kspace, line_index).reshape(SLABS, PAIRS * ROWS, 128)
    arrived = lax.all_to_all(sent, "slab", split_axis=0, concat_axis=0, tiled=True)
    return combine(images(arrived, coil_maps))


def solution(mesh):
    placed = (
        P(None, "coil", None, None, "slab", None),
        P(None, "coil", None, "slab", None),
        P(None, "slab", None),
    )
    return jax.shard_map(
        local, mesh=mesh, in_specs=placed, out_specs=P("coil", None, "slab", None), check_vma=False
    )
```

```python
import functools
import math

import jax
import jax.numpy as jnp
import numpy as np
from jax import lax
from jax.experimental import pallas as pl
from jax.experimental.pallas import tpu as pltpu
from jax.sharding import Mesh
from jax.sharding import PartitionSpec as P

NY = 384
NZ = 384
PHASES = 8
SLABS = 32
YL = NY // SLABS
KZL = NZ // SLABS
CX = 4
XL = 8
BLOCK = 3 * KZL
SENT = CX * SLABS * BLOCK


def dft(rows, cols, length):
    turns = np.outer(rows, cols) % length
    angles = turns * (2.0 * math.pi / length)
    scaling = 1.0 / math.sqrt(length)
    return np.cos(angles) * scaling, np.sin(angles) * scaling


@functools.cache
def row_table():
    y = np.arange(YL)[:, None] + np.arange(SLABS)[None, :] * YL
    return np.concatenate(dft(y.reshape(-1), np.arange(NY), NY), axis=1).astype(jnp.bfloat16)


@functools.cache
def depth_table():
    kz = (np.arange(KZL)[:, None] + np.arange(SLABS)[None, :] * KZL).reshape(-1)
    cosine, sine = dft(kz, np.arange(NZ), NZ)
    from_real = np.concatenate([cosine, sine], axis=1)
    from_imag = np.concatenate([-sine, cosine], axis=1)
    return np.concatenate([from_real, from_imag], axis=0).astype(jnp.bfloat16)


def encode_kernel(k_ref, line_ref, w_ref, out_ref, scratch):
    theta = 2.0 * math.pi / PHASES
    cosine = math.cos(theta)
    sine = math.sin(theta)
    ky = lax.broadcasted_iota(jnp.int32, (NY, 128), 0)
    lanes = lax.broadcasted_iota(jnp.int32, (1, 128), 1)

    def grid_of(kz):
        early_re, early_im, late_re, late_im = (
            jnp.concatenate([k_ref[part, c, t, kz] for c in range(2)], axis=0)
            for t in range(2)
            for part in range(2)
        )
        late_re = late_re.astype(jnp.float32)
        late_im = late_im.astype(jnp.float32)
        turned_re = (cosine * late_re + sine * late_im).astype(jnp.bfloat16)
        turned_im = (cosine * late_im - sine * late_re).astype(jnp.bfloat16)
        early = jnp.concatenate([early_re, early_im, -early_im, early_re], axis=0)
        late = jnp.concatenate([turned_re, turned_im, -turned_im, turned_re], axis=0)
        samples = jnp.concatenate([early, late], axis=1)
        chosen = jnp.concatenate(
            [jnp.where(ky == line_ref[kz, t : t + 1, :], 1.0, 0.0).astype(jnp.bfloat16) for t in range(2)],
            axis=1,
        )
        placed = lax.dot_general(
            chosen, samples, (((1,), (1,)), ((), ())), preferred_element_type=jnp.float32
        ).astype(jnp.bfloat16)
        return jnp.concatenate([placed[:, :128], placed[:, 128:]], axis=0)

    def exchange(a, b, bit):
        upper = (lanes & bit) != 0
        return (
            jnp.where(upper, pltpu.roll(b, bit, 1), a),
            jnp.where(upper, b, pltpu.roll(a, 128 - bit, 1)),
        )

    for pair in range(KZL // 2):
        grids = jnp.concatenate([grid_of(2 * pair), grid_of(2 * pair + 1)], axis=1)
        both = jnp.dot(w_ref[...], grids, preferred_element_type=jnp.float32)
        for half in range(2):
            kz = 2 * pair + half
            for third in range(3):
                part = both[third * 128 : third * 128 + 128, half * 128 : half * 128 + 128]
                for high, sides in enumerate(exchange(part[:64], part[64:], 16)):
                    for low, value in enumerate(exchange(sides[:32], sides[32:], 8)):
                        start = (2 * high + low) * SLABS * BLOCK + third * KZL + kz
                        scratch[pl.ds(start, SLABS, stride=BLOCK), :] = value
    out_ref[...] = scratch[...].astype(jnp.bfloat16)


def encode(kspace, line_index):
    return pl.pallas_call(
        encode_kernel,
        out_shape=jax.ShapeDtypeStruct((SENT, 128), jnp.bfloat16),
        in_specs=[pl.BlockSpec(memory_space=pltpu.VMEM)] * 3,
        out_specs=pl.BlockSpec(memory_space=pltpu.VMEM),
        scratch_shapes=[pltpu.VMEM((SENT, 128), jnp.float32)],
        name="encode",
    )(jnp.transpose(kspace, (0, 1, 2, 4, 3, 5)), jnp.transpose(line_index, (1, 0, 2)), jnp.asarray(row_table()))


def image_kernel(me_ref, r_ref, m0_ref, m1_ref, m2_ref, m3_ref, d_ref, own_ref, other_ref, wide, lhs, sums):
    wide[...] = r_ref[...].astype(jnp.float32)
    column = me_ref[0]
    core = me_ref[1]
    for step in range(CX):
        base = (column ^ step) * (SLABS * BLOCK)
        for third in range(3):
            rows = jnp.concatenate(
                [wide[pl.ds(base + third * KZL + kz, SLABS, stride=BLOCK), :] for kz in range(KZL)], axis=0
            )
            turned = rows.T.astype(jnp.bfloat16)
            at = (step * 3 + third) * 64
            lhs[at : at + 64, : KZL * SLABS] = turned[:64]
            lhs[at : at + 64, KZL * SLABS :] = turned[64:]
    image = jnp.dot(lhs[...], d_ref[...], preferred_element_type=jnp.float32)
    for third in range(3):
        real = imag = None
        for step, m_ref in enumerate((m0_ref, m1_ref, m2_ref, m3_ref)):
            for c in range(2):
                at = (step * 3 + third) * 64 + c * 32
                image_re = image[at : at + 32, :NZ]
                image_im = image[at : at + 32, NZ:]
                map_re, map_im = (
                    m_ref[part, c, 4 * third : 4 * third + 4].astype(jnp.float32).reshape(32, NZ) for part in range(2)
                )
                add_re = map_re * image_re + map_im * image_im
                add_im = map_re * image_im - map_im * image_re
                real, imag = (add_re, add_im) if real is None else (real + add_re, imag + add_im)
        for part, value in enumerate((real, imag)):
            for y in range(4):
                for lane in range(3):
                    sums[lane, pl.ds(2 * (4 * third + y) + part, XL, stride=2 * YL), :] = value[
                        y * 8 : y * 8 + 8, lane * 128 : lane * 128 + 128
                    ]
    rows = 4 * YL
    for zh in range(2):
        for lane in range(3):
            at = slice(lane * 128, lane * 128 + 128)
            own_ref[zh * rows : zh * rows + rows, at] = sums[lane, pl.ds((2 * zh + core) * rows, rows), :]
            other_ref[zh * rows : zh * rows + rows, at] = sums[lane, pl.ds((2 * zh + 1 - core) * rows, rows), :]


def images(arrived, maps):
    me = jnp.stack([lax.axis_index("cx"), lax.axis_index("core")]).astype(jnp.int32)
    vmem = pl.BlockSpec(memory_space=pltpu.VMEM)
    half = jax.ShapeDtypeStruct((8 * YL, NZ), jnp.float32)
    return pl.pallas_call(
        image_kernel,
        out_shape=(half, half),
        in_specs=[pl.BlockSpec(memory_space=pltpu.SMEM)] + [vmem] * 6,
        out_specs=(vmem, vmem),
        scratch_shapes=[
            pltpu.VMEM((SENT, 128), jnp.float32),
            pltpu.VMEM((2 * NZ, 2 * NZ), jnp.bfloat16),
            pltpu.VMEM((3, 2 * YL * XL, 128), jnp.float32),
        ],
        name="images",
    )(me, arrived, *maps, jnp.asarray(depth_table()))


def shared_maps(coil_maps):
    rows = jnp.transpose(coil_maps, (0, 1, 3, 2, 4))
    column = lax.axis_index("cx")
    chunks = []
    for step in range(CX):
        chunk = lax.dynamic_slice_in_dim(rows, (column ^ step) * XL, XL, axis=3)
        if step:
            chunk = lax.ppermute(chunk, "cx", [(i, i ^ step) for i in range(CX)])
        chunks.append(chunk)
    return chunks


def local(kspace, coil_maps, line_index):
    sent, coil_maps = lax.optimization_barrier((encode(kspace, line_index), coil_maps))
    arrived = lax.all_to_all(
        sent.reshape(CX * SLABS, BLOCK // 4, 4, 128), ("cx", "slab"), split_axis=0, concat_axis=0, tiled=True
    ).reshape(SENT, 128)
    own, other = images(arrived, shared_maps(coil_maps))
    swap = [(0, 1), (1, 0)]
    pairs = (own + lax.ppermute(other, "core", swap)).reshape(2, 4 * YL, NZ)
    far = lax.axis_index("zh")
    own = lax.dynamic_index_in_dim(pairs, far, 0, keepdims=False)
    other = lax.dynamic_index_in_dim(pairs, 1 - far, 0, keepdims=False)
    total = own + lax.ppermute(other, "zh", swap)
    return jnp.transpose(total.reshape(2, YL, 2, NZ), (0, 2, 1, 3))


def solution(mesh):
    fine = Mesh(mesh.devices.reshape(CX, 2, 2, SLABS), ("cx", "zh", "core", "slab"))
    coil = ("cx", "zh", "core")
    placed = (
        P(None, coil, None, None, "slab", None),
        P(None, coil, None, "slab", None),
        P(None, "slab", None),
    )
    return jax.shard_map(
        local, mesh=fine, in_specs=placed, out_specs=P(coil, None, "slab", None), check_vma=False
    )
```

```python
import functools
import math

import jax
import jax.numpy as jnp
import numpy as np
from jax import lax
from jax.experimental import pallas as pl
from jax.experimental.pallas import tpu as pltpu
from jax.sharding import Mesh
from jax.sharding import PartitionSpec as P

NY = 384
NZ = 384
PHASES = 8
SLABS = 32
YL = NY // SLABS
KZL = NZ // SLABS
CX = 4
XL = 8
BLOCK = 3 * KZL
SENT = CX * SLABS * BLOCK


def dft(rows, cols, length):
    turns = np.outer(rows, cols) % length
    angles = turns * (2.0 * math.pi / length)
    scaling = 1.0 / math.sqrt(length)
    return np.cos(angles) * scaling, np.sin(angles) * scaling


@functools.cache
def row_table():
    y = np.arange(YL)[:, None] + np.arange(SLABS)[None, :] * YL
    return np.concatenate(dft(y.reshape(-1), np.arange(NY), NY), axis=1).astype(jnp.bfloat16)


@functools.cache
def depth_table():
    kz = (np.arange(KZL)[:, None] + np.arange(SLABS)[None, :] * KZL).reshape(-1)
    cosine, sine = dft(kz, np.arange(NZ), NZ)
    from_real = np.concatenate([cosine, sine], axis=1)
    from_imag = np.concatenate([-sine, cosine], axis=1)
    return np.concatenate([from_real, from_imag], axis=0).astype(jnp.bfloat16)


def encode_kernel(k_ref, line_ref, w_ref, out_ref, scratch):
    theta = 2.0 * math.pi / PHASES
    cosine = math.cos(theta)
    sine = math.sin(theta)
    ky = lax.broadcasted_iota(jnp.int32, (NY, 128), 0)
    lanes = lax.broadcasted_iota(jnp.int32, (1, 128), 1)

    def grid_of(kz):
        early_re, early_im, late_re, late_im = (
            jnp.concatenate([k_ref[part, c, t, kz] for c in range(2)], axis=0)
            for t in range(2)
            for part in range(2)
        )
        late_re = late_re.astype(jnp.float32)
        late_im = late_im.astype(jnp.float32)
        turned_re = (cosine * late_re + sine * late_im).astype(jnp.bfloat16)
        turned_im = (cosine * late_im - sine * late_re).astype(jnp.bfloat16)
        early = jnp.concatenate([early_re, early_im, -early_im, early_re], axis=0)
        late = jnp.concatenate([turned_re, turned_im, -turned_im, turned_re], axis=0)
        samples = jnp.concatenate([early, late], axis=1)
        chosen = jnp.concatenate(
            [jnp.where(ky == line_ref[kz, t : t + 1, :], 1.0, 0.0).astype(jnp.bfloat16) for t in range(2)],
            axis=1,
        )
        placed = lax.dot_general(
            chosen, samples, (((1,), (1,)), ((), ())), preferred_element_type=jnp.float32
        ).astype(jnp.bfloat16)
        return jnp.concatenate([placed[:, :128], placed[:, 128:]], axis=0)

    def exchange(a, b, bit):
        upper = (lanes & bit) != 0
        return (
            jnp.where(upper, pltpu.roll(b, bit, 1), a),
            jnp.where(upper, b, pltpu.roll(a, 128 - bit, 1)),
        )

    for pair in range(KZL // 2):
        grids = jnp.concatenate([grid_of(2 * pair), grid_of(2 * pair + 1)], axis=1)
        both = jnp.dot(w_ref[...], grids, preferred_element_type=jnp.float32)
        for half in range(2):
            kz = 2 * pair + half
            for third in range(3):
                part = both[third * 128 : third * 128 + 128, half * 128 : half * 128 + 128]
                for high, sides in enumerate(exchange(part[:64], part[64:], 16)):
                    for low, value in enumerate(exchange(sides[:32], sides[32:], 8)):
                        start = (2 * high + low) * SLABS * BLOCK + third * KZL + kz
                        scratch[pl.ds(start, SLABS, stride=BLOCK), :] = value
    out_ref[...] = scratch[...].astype(jnp.bfloat16)


def encode(kspace, line_index):
    return pl.pallas_call(
        encode_kernel,
        out_shape=jax.ShapeDtypeStruct((SENT, 128), jnp.bfloat16),
        in_specs=[pl.BlockSpec(memory_space=pltpu.VMEM)] * 3,
        out_specs=pl.BlockSpec(memory_space=pltpu.VMEM),
        scratch_shapes=[pltpu.VMEM((SENT, 128), jnp.float32)],
        name="encode",
    )(jnp.transpose(kspace, (0, 1, 2, 4, 3, 5)), jnp.transpose(line_index, (1, 0, 2)), jnp.asarray(row_table()))


def image_kernel(me_ref, r_ref, m0_ref, m1_ref, m2_ref, m3_ref, d_ref, own_ref, other_ref, wide, lhs, sums):
    wide[...] = r_ref[...].astype(jnp.float32)
    column = me_ref[0]
    core = me_ref[1]
    for step in range(CX):
        base = (column ^ step) * (SLABS * BLOCK)
        for third in range(3):
            rows = jnp.concatenate(
                [wide[pl.ds(base + third * KZL + kz, SLABS, stride=BLOCK), :] for kz in range(KZL)], axis=0
            )
            turned = rows.T.astype(jnp.bfloat16)
            at = (step * 3 + third) * 64
            lhs[at : at + 64, : KZL * SLABS] = turned[:64]
            lhs[at : at + 64, KZL * SLABS :] = turned[64:]
    image = jnp.dot(lhs[...], d_ref[...], preferred_element_type=jnp.float32)
    for third in range(3):
        real = imag = None
        for step, m_ref in enumerate((m0_ref, m1_ref, m2_ref, m3_ref)):
            for c in range(2):
                at = (step * 3 + third) * 64 + c * 32
                image_re = image[at : at + 32, :NZ]
                image_im = image[at : at + 32, NZ:]
                map_re, map_im = (
                    m_ref[part, c, 4 * third : 4 * third + 4].astype(jnp.float32).reshape(32, NZ) for part in range(2)
                )
                add_re = map_re * image_re + map_im * image_im
                add_im = map_re * image_im - map_im * image_re
                real, imag = (add_re, add_im) if real is None else (real + add_re, imag + add_im)
        for part, value in enumerate((real, imag)):
            for y in range(4):
                for lane in range(3):
                    sums[lane, pl.ds(2 * (4 * third + y) + part, XL, stride=2 * YL), :] = value[
                        y * 8 : y * 8 + 8, lane * 128 : lane * 128 + 128
                    ]
    rows = 4 * YL
    for zh in range(2):
        for lane in range(3):
            at = slice(lane * 128, lane * 128 + 128)
            own_ref[zh * rows : zh * rows + rows, at] = sums[lane, pl.ds((2 * zh + core) * rows, rows), :]
            other_ref[zh * rows : zh * rows + rows, at] = sums[lane, pl.ds((2 * zh + 1 - core) * rows, rows), :]


def images(arrived, maps):
    me = jnp.stack([lax.axis_index("cx"), lax.axis_index("core")]).astype(jnp.int32)
    vmem = pl.BlockSpec(memory_space=pltpu.VMEM)
    half = jax.ShapeDtypeStruct((8 * YL, NZ), jnp.float32)
    return pl.pallas_call(
        image_kernel,
        out_shape=(half, half),
        in_specs=[pl.BlockSpec(memory_space=pltpu.SMEM)] + [vmem] * 6,
        out_specs=(vmem, vmem),
        scratch_shapes=[
            pltpu.VMEM((SENT, 128), jnp.float32),
            pltpu.VMEM((2 * NZ, 2 * NZ), jnp.bfloat16),
            pltpu.VMEM((3, 2 * YL * XL, 128), jnp.float32),
        ],
        name="images",
    )(me, *(pltpu.with_memory_space_constraint(x, pltpu.VMEM) for x in (arrived, *maps, jnp.asarray(depth_table()))))


def shared_maps(coil_maps):
    rows = jnp.transpose(coil_maps, (0, 1, 3, 2, 4))
    column = lax.axis_index("cx")
    chunks = []
    for step in range(CX):
        chunk = lax.dynamic_slice_in_dim(rows, (column ^ step) * XL, XL, axis=3)
        if step:
            chunk = lax.ppermute(chunk, "cx", [(i, i ^ step) for i in range(CX)])
        chunks.append(chunk)
    return chunks


def from_partner(value, axis):
    pair = lax.all_gather(value, axis)
    return lax.dynamic_index_in_dim(pair, 1 - lax.axis_index(axis), 0, keepdims=False)


def local(kspace, coil_maps, line_index):
    sent, coil_maps = lax.optimization_barrier((encode(kspace, line_index), coil_maps))
    arrived = lax.all_to_all(
        sent.reshape(CX * SLABS, BLOCK // 4, 4, 128), ("cx", "slab"), split_axis=0, concat_axis=0, tiled=True
    ).reshape(SENT, 128)
    own, other = images(arrived, shared_maps(coil_maps))
    pairs = (own + from_partner(other, "core")).reshape(2, 4 * YL, NZ)
    far = lax.axis_index("zh")
    own = lax.dynamic_index_in_dim(pairs, far, 0, keepdims=False)
    other = lax.dynamic_index_in_dim(pairs, 1 - far, 0, keepdims=False)
    total = own + from_partner(other.astype(jnp.bfloat16), "zh").astype(jnp.float32)
    return jnp.transpose(total.reshape(2, YL, 2, NZ), (0, 2, 1, 3))


def solution(mesh):
    fine = Mesh(mesh.devices.reshape(CX, 2, 2, SLABS), ("cx", "zh", "core", "slab"))
    coil = ("cx", "zh", "core")
    placed = (
        P(None, coil, None, None, "slab", None),
        P(None, coil, None, "slab", None),
        P(None, "slab", None),
    )
    return jax.shard_map(
        local, mesh=fine, in_specs=placed, out_specs=P(coil, None, "slab", None), check_vma=False
    )
```

```python
import functools
import math

import jax
import jax.numpy as jnp
import numpy as np
from jax import lax
from jax.experimental import pallas as pl
from jax.experimental.pallas import tpu as pltpu
from jax.sharding import Mesh
from jax.sharding import PartitionSpec as P

NY = 384
NZ = 384
PHASES = 8
SLABS = 32
YL = NY // SLABS
KZL = NZ // SLABS
CX = 4
XL = 8
BLOCK = 3 * KZL
SENT = CX * SLABS * BLOCK


def dft(rows, cols, length):
    turns = np.outer(rows, cols) % length
    angles = turns * (2.0 * math.pi / length)
    scaling = 1.0 / math.sqrt(length)
    return np.cos(angles) * scaling, np.sin(angles) * scaling


@functools.cache
def row_table():
    y = np.arange(YL)[:, None] + np.arange(SLABS)[None, :] * YL
    return np.concatenate(dft(y.reshape(-1), np.arange(NY), NY), axis=1).astype(jnp.bfloat16)


@functools.cache
def depth_table():
    kz = (np.arange(KZL)[:, None] + np.arange(SLABS)[None, :] * KZL).reshape(-1)
    cosine, sine = dft(kz, np.arange(NZ), NZ)
    from_real = np.concatenate([cosine, sine], axis=1)
    from_imag = np.concatenate([-sine, cosine], axis=1)
    return np.concatenate([from_real, from_imag], axis=0).astype(jnp.bfloat16)


def encode_kernel(k_ref, line_ref, w_ref, out_ref, scratch):
    theta = 2.0 * math.pi / PHASES
    cosine = math.cos(theta)
    sine = math.sin(theta)
    ky = lax.broadcasted_iota(jnp.int32, (NY, 128), 0)
    lanes = lax.broadcasted_iota(jnp.int32, (1, 128), 1)

    def grid_of(kz):
        early_re, early_im, late_re, late_im = (
            jnp.concatenate([k_ref[part, c, t, kz] for c in range(2)], axis=0)
            for t in range(2)
            for part in range(2)
        )
        late_re = late_re.astype(jnp.float32)
        late_im = late_im.astype(jnp.float32)
        turned_re = (cosine * late_re + sine * late_im).astype(jnp.bfloat16)
        turned_im = (cosine * late_im - sine * late_re).astype(jnp.bfloat16)
        early = jnp.concatenate([early_re, early_im, -early_im, early_re], axis=0)
        late = jnp.concatenate([turned_re, turned_im, -turned_im, turned_re], axis=0)
        samples = jnp.concatenate([early, late], axis=1)
        chosen = jnp.concatenate(
            [jnp.where(ky == line_ref[kz, t : t + 1, :], 1.0, 0.0).astype(jnp.bfloat16) for t in range(2)],
            axis=1,
        )
        placed = lax.dot_general(
            chosen, samples, (((1,), (1,)), ((), ())), preferred_element_type=jnp.float32
        ).astype(jnp.bfloat16)
        return jnp.concatenate([placed[:, :128], placed[:, 128:]], axis=0)

    def exchange(a, b, bit):
        upper = (lanes & bit) != 0
        return (
            jnp.where(upper, pltpu.roll(b, bit, 1), a),
            jnp.where(upper, b, pltpu.roll(a, 128 - bit, 1)),
        )

    for pair in range(KZL // 2):
        grids = jnp.concatenate([grid_of(2 * pair), grid_of(2 * pair + 1)], axis=1)
        both = jnp.dot(w_ref[...], grids, preferred_element_type=jnp.float32)
        for half in range(2):
            kz = 2 * pair + half
            for third in range(3):
                part = both[third * 128 : third * 128 + 128, half * 128 : half * 128 + 128].astype(jnp.bfloat16)
                for high, sides in enumerate(exchange(part[:64], part[64:], 16)):
                    for low, value in enumerate(exchange(sides[:32], sides[32:], 8)):
                        start = (2 * high + low) * SLABS * BLOCK + third * KZL + kz
                        scratch[pl.ds(start, SLABS, stride=BLOCK), :] = value.astype(jnp.float32)
    out_ref[...] = scratch[...].astype(jnp.bfloat16)


def encode(kspace, line_index):
    return pl.pallas_call(
        encode_kernel,
        out_shape=jax.ShapeDtypeStruct((SENT, 128), jnp.bfloat16),
        in_specs=[pl.BlockSpec(memory_space=pltpu.VMEM)] * 3,
        out_specs=pl.BlockSpec(memory_space=pltpu.VMEM),
        scratch_shapes=[pltpu.VMEM((SENT, 128), jnp.float32)],
        name="encode",
    )(jnp.transpose(kspace, (0, 1, 2, 4, 3, 5)), jnp.transpose(line_index, (1, 0, 2)), jnp.asarray(row_table()))


def image_kernel(me_ref, r_ref, m0_ref, m1_ref, m2_ref, m3_ref, d_ref, own_ref, other_ref, wide, lhs, sums):
    wide[...] = r_ref[...].astype(jnp.float32)
    column = me_ref[0]
    core = me_ref[1]
    for third in range(3):
        for step in range(CX):
            base = (column ^ step) * (SLABS * BLOCK)
            rows = jnp.concatenate(
                [wide[pl.ds(base + third * KZL + kz, SLABS, stride=BLOCK), :] for kz in range(KZL)], axis=0
            )
            turned = rows.T.astype(jnp.bfloat16)
            lhs[third, step * 64 : step * 64 + 64, : KZL * SLABS] = turned[:64]
            lhs[third, step * 64 : step * 64 + 64, KZL * SLABS :] = turned[64:]
        image = jnp.dot(lhs[third], d_ref[...], preferred_element_type=jnp.float32)
        real = imag = None
        for step, m_ref in enumerate((m0_ref, m1_ref, m2_ref, m3_ref)):
            for c in range(2):
                at = step * 64 + c * 32
                image_re = image[at : at + 32, :NZ]
                image_im = image[at : at + 32, NZ:]
                map_re, map_im = (
                    m_ref[part, c, 4 * third : 4 * third + 4].astype(jnp.float32).reshape(32, NZ) for part in range(2)
                )
                add_re = map_re * image_re + map_im * image_im
                add_im = map_re * image_im - map_im * image_re
                real, imag = (add_re, add_im) if real is None else (real + add_re, imag + add_im)
        for part, value in enumerate((real, imag)):
            for y in range(4):
                for lane in range(3):
                    sums[lane, pl.ds(2 * (4 * third + y) + part, XL, stride=2 * YL), :] = value[
                        y * 8 : y * 8 + 8, lane * 128 : lane * 128 + 128
                    ]
    rows = 4 * YL
    for zh in range(2):
        for lane in range(3):
            at = slice(lane * 128, lane * 128 + 128)
            own_ref[zh * rows : zh * rows + rows, at] = sums[lane, pl.ds((2 * zh + core) * rows, rows), :]
            other_ref[zh * rows : zh * rows + rows, at] = sums[lane, pl.ds((2 * zh + 1 - core) * rows, rows), :]


def images(arrived, maps):
    me = jnp.stack([lax.axis_index("cx"), lax.axis_index("core")]).astype(jnp.int32)
    vmem = pl.BlockSpec(memory_space=pltpu.VMEM)
    half = jax.ShapeDtypeStruct((8 * YL, NZ), jnp.float32)
    return pl.pallas_call(
        image_kernel,
        out_shape=(half, half),
        in_specs=[pl.BlockSpec(memory_space=pltpu.SMEM)] + [vmem] * 6,
        out_specs=(vmem, vmem),
        scratch_shapes=[
            pltpu.VMEM((SENT, 128), jnp.float32),
            pltpu.VMEM((3, 4 * 64, 2 * NZ), jnp.bfloat16),
            pltpu.VMEM((3, 2 * YL * XL, 128), jnp.float32),
        ],
        compiler_params=pltpu.CompilerParams(vmem_limit_bytes=24 << 20),
        name="images",
    )(me, *(pltpu.with_memory_space_constraint(x, pltpu.VMEM) for x in (arrived, *maps, jnp.asarray(depth_table()))))


def shared_maps(coil_maps):
    rows = jnp.transpose(coil_maps, (0, 1, 3, 2, 4))
    column = lax.axis_index("cx")
    chunks = []
    for step in range(CX):
        chunk = lax.dynamic_slice_in_dim(rows, (column ^ step) * XL, XL, axis=3)
        if step:
            chunk = lax.ppermute(chunk, "cx", [(i, i ^ step) for i in range(CX)])
        chunks.append(chunk)
    return chunks


def from_partner(value, axis):
    pair = lax.all_gather(value, axis)
    return lax.dynamic_index_in_dim(pair, 1 - lax.axis_index(axis), 0, keepdims=False)


def local(kspace, coil_maps, line_index):
    sent, coil_maps = lax.optimization_barrier((encode(kspace, line_index), coil_maps))
    arrived = lax.all_to_all(
        sent.reshape(CX * SLABS, BLOCK // 4, 4, 128), ("cx", "slab"), split_axis=0, concat_axis=0, tiled=True
    ).reshape(SENT, 128)
    own, other = images(arrived, shared_maps(coil_maps))
    pairs = (own + from_partner(other, "core")).reshape(2, 4 * YL, NZ)
    far = lax.axis_index("zh")
    own = lax.dynamic_index_in_dim(pairs, far, 0, keepdims=False)
    other = lax.dynamic_index_in_dim(pairs, 1 - far, 0, keepdims=False)
    total = own + from_partner(other.astype(jnp.bfloat16), "zh").astype(jnp.float32)
    return jnp.transpose(total.reshape(2, YL, 2, NZ), (0, 2, 1, 3))


def solution(mesh):
    fine = Mesh(mesh.devices.reshape(CX, 2, 2, SLABS), ("cx", "zh", "core", "slab"))
    coil = ("cx", "zh", "core")
    placed = (
        P(None, coil, None, None, "slab", None),
        P(None, coil, None, "slab", None),
        P(None, "slab", None),
    )
    return jax.shard_map(
        local, mesh=fine, in_specs=placed, out_specs=P(coil, None, "slab", None), check_vma=False
    )
```

```python
import functools
import math

import jax
import jax.numpy as jnp
import numpy as np
from jax import lax
from jax.experimental import pallas as pl
from jax.experimental.pallas import tpu as pltpu
from jax.sharding import Mesh
from jax.sharding import PartitionSpec as P

NY = 384
NZ = 384
PHASES = 8
SLABS = 32
YL = NY // SLABS
KZL = NZ // SLABS
CX = 4
XL = 8
BLOCK = 3 * KZL
QUARTER = NY // 4
SENT = CX * SLABS * BLOCK
PADDED = SENT + 40


def dft(rows, cols, length):
    turns = np.outer(rows, cols) % length
    angles = turns * (2.0 * math.pi / length)
    scaling = 1.0 / math.sqrt(length)
    return np.cos(angles) * scaling, np.sin(angles) * scaling


@functools.cache
def row_table():
    y = (np.arange(YL)[:, None] + np.arange(SLABS // 4)[None, :] * YL).reshape(-1)
    parts = [np.concatenate(dft(y, np.arange(residue, NY, 4), NY), axis=1) for residue in range(4)]
    return np.stack(parts).astype(jnp.bfloat16)


@functools.cache
def depth_table():
    kz = (np.arange(KZL)[:, None] + np.arange(SLABS)[None, :] * KZL).reshape(-1)
    cosine, sine = dft(kz, np.arange(NZ), NZ)
    from_real = np.concatenate([cosine, sine], axis=1)
    from_imag = np.concatenate([-sine, cosine], axis=1)
    return np.concatenate([from_real, from_imag], axis=0).astype(jnp.bfloat16)


def encode_kernel(k_ref, line_ref, w_ref, out_ref, scratch):
    theta = 2.0 * math.pi / PHASES
    cosine = math.cos(theta)
    sine = math.sin(theta)
    row = lax.broadcasted_iota(jnp.int32, (NY, 128), 0)
    ky = 4 * (row % QUARTER) + row // QUARTER
    lanes = lax.broadcasted_iota(jnp.int32, (1, 128), 1)

    def grid_of(kz):
        early_re, early_im, late_re, late_im = (
            jnp.concatenate([k_ref[part, c, t, kz] for c in range(2)], axis=0)
            for t in range(2)
            for part in range(2)
        )
        late_re = late_re.astype(jnp.float32)
        late_im = late_im.astype(jnp.float32)
        turned_re = (cosine * late_re + sine * late_im).astype(jnp.bfloat16)
        turned_im = (cosine * late_im - sine * late_re).astype(jnp.bfloat16)
        early = jnp.concatenate([early_re, early_im, -early_im, early_re], axis=0)
        late = jnp.concatenate([turned_re, turned_im, -turned_im, turned_re], axis=0)
        samples = jnp.concatenate([early, late], axis=1)
        chosen = jnp.concatenate(
            [jnp.where(ky == line_ref[kz, t : t + 1, :], 1.0, 0.0).astype(jnp.bfloat16) for t in range(2)],
            axis=1,
        )
        placed = lax.dot_general(
            chosen, samples, (((1,), (1,)), ((), ())), preferred_element_type=jnp.float32
        ).astype(jnp.bfloat16)
        return [
            jnp.concatenate([placed[at : at + QUARTER, :128], placed[at : at + QUARTER, 128:]], axis=0)
            for at in range(0, NY, QUARTER)
        ]

    def exchange(a, b, bit):
        upper = (lanes & bit) != 0
        return (
            jnp.where(upper, pltpu.roll(b, bit, 1), a),
            jnp.where(upper, b, pltpu.roll(a, 128 - bit, 1)),
        )

    sign = jnp.where(lanes < 64, -1.0, 1.0)

    ahead = grid_of(0), grid_of(1)
    for pair in range(KZL // 2):
        first, second = ahead
        if pair + 1 < KZL // 2:
            ahead = grid_of(2 * pair + 2), grid_of(2 * pair + 3)
        both = [
            jnp.dot(w_ref[residue], jnp.concatenate([first[residue], second[residue]], axis=1), preferred_element_type=jnp.float32)
            for residue in range(4)
        ]
        for half in range(2):
            kz = 2 * pair + half
            f0, f1, f2, f3 = (part[:, half * 128 : half * 128 + 128] for part in both)
            even, odd = f0 + f2, f1 + f3
            cross, turned = f0 - f2, sign * pltpu.roll(f1 - f3, 64, 1)
            quarters = (even + odd, cross + turned, even - odd, cross - turned)
            for side in range(2):
                for third in range(3):
                    tiles = []
                    for y in range(4 * third, 4 * third + 4):
                        near, far = (q[8 * y : 8 * y + 8] for q in quarters[2 * side : 2 * side + 2])
                        tiles.append(jnp.concatenate([near, far], axis=0).astype(jnp.bfloat16))
                    low = exchange(tiles[0], tiles[2], 16)
                    high = exchange(tiles[1], tiles[3], 16)
                    for upper in range(2):
                        for lower, value in enumerate(exchange(low[upper], high[upper], 8)):
                            start = ((2 * upper + lower) * SLABS + 16 * side) * BLOCK + third * KZL + kz
                            scratch[pl.ds(start, 16, stride=BLOCK), :] = value.astype(jnp.float32)
    out_ref[...] = scratch[:SENT].astype(jnp.bfloat16)


def encode(kspace, line_index):
    return pl.pallas_call(
        encode_kernel,
        out_shape=jax.ShapeDtypeStruct((SENT, 128), jnp.bfloat16),
        in_specs=[pl.BlockSpec(memory_space=pltpu.VMEM)] * 3,
        out_specs=pl.BlockSpec(memory_space=pltpu.VMEM),
        scratch_shapes=[pltpu.VMEM((PADDED, 128), jnp.float32)],
        name="encode",
    )(jnp.transpose(kspace, (0, 1, 2, 4, 3, 5)), jnp.transpose(line_index, (1, 0, 2)), jnp.asarray(row_table()))


def image_kernel(me_ref, r_ref, m0_ref, m1_ref, m2_ref, m3_ref, d_ref, own_ref, other_ref, wide, lhs, sums):
    wide[:SENT] = r_ref[...].astype(jnp.float32)
    column = me_ref[0]
    core = me_ref[1]
    for third in range(3):
        for step in range(CX):
            base = (column ^ step) * (SLABS * BLOCK)
            rows = jnp.concatenate(
                [wide[pl.ds(base + third * KZL + kz, SLABS, stride=BLOCK), :] for kz in range(KZL)], axis=0
            )
            turned = rows.T.astype(jnp.bfloat16)
            lhs[third, step * 64 : step * 64 + 64, : KZL * SLABS] = turned[:64]
            lhs[third, step * 64 : step * 64 + 64, KZL * SLABS :] = turned[64:]
        image = jnp.dot(lhs[third], d_ref[...], preferred_element_type=jnp.float32)
        real = imag = None
        for step, m_ref in enumerate((m0_ref, m1_ref, m2_ref, m3_ref)):
            for c in range(2):
                at = step * 64 + c * 32
                image_re = image[at : at + 32, :NZ]
                image_im = image[at : at + 32, NZ:]
                map_re, map_im = (
                    m_ref[part, c, 4 * third : 4 * third + 4].astype(jnp.float32).reshape(32, NZ) for part in range(2)
                )
                add_re = map_re * image_re + map_im * image_im
                add_im = map_re * image_im - map_im * image_re
                real, imag = (add_re, add_im) if real is None else (real + add_re, imag + add_im)
        for part, value in enumerate((real, imag)):
            for y in range(4):
                for lane in range(3):
                    sums[lane, pl.ds(2 * (4 * third + y) + part, XL, stride=2 * YL), :] = value[
                        y * 8 : y * 8 + 8, lane * 128 : lane * 128 + 128
                    ]
    rows = 4 * YL
    for zh in range(2):
        for lane in range(3):
            at = slice(lane * 128, lane * 128 + 128)
            own_ref[zh * rows : zh * rows + rows, at] = sums[lane, pl.ds((2 * zh + core) * rows, rows), :]
            other_ref[zh * rows : zh * rows + rows, at] = sums[lane, pl.ds((2 * zh + 1 - core) * rows, rows), :]


def images(arrived, maps):
    me = jnp.stack([lax.axis_index("cx"), lax.axis_index("core")]).astype(jnp.int32)
    vmem = pl.BlockSpec(memory_space=pltpu.VMEM)
    half = jax.ShapeDtypeStruct((8 * YL, NZ), jnp.float32)
    return pl.pallas_call(
        image_kernel,
        out_shape=(half, half),
        in_specs=[pl.BlockSpec(memory_space=pltpu.SMEM)] + [vmem] * 6,
        out_specs=(vmem, vmem),
        scratch_shapes=[
            pltpu.VMEM((PADDED, 128), jnp.float32),
            pltpu.VMEM((3, 4 * 64, 2 * NZ), jnp.bfloat16),
            pltpu.VMEM((3, 2 * YL * (XL + 1), 128), jnp.float32),
        ],
        compiler_params=pltpu.CompilerParams(vmem_limit_bytes=24 << 20),
        name="images",
    )(me, *(pltpu.with_memory_space_constraint(x, pltpu.VMEM) for x in (arrived, *maps, jnp.asarray(depth_table()))))


def shared_maps(coil_maps):
    rows = jnp.transpose(coil_maps, (0, 1, 3, 2, 4))
    column = lax.axis_index("cx")
    chunks = []
    for step in range(CX):
        chunk = lax.dynamic_slice_in_dim(rows, (column ^ step) * XL, XL, axis=3)
        if step:
            chunk = lax.ppermute(chunk, "cx", [(i, i ^ step) for i in range(CX)])
        chunks.append(chunk)
    return chunks


def from_partner(value, axis):
    pair = lax.all_gather(value, axis)
    return lax.dynamic_index_in_dim(pair, 1 - lax.axis_index(axis), 0, keepdims=False)


def local(kspace, coil_maps, line_index):
    sent, coil_maps = lax.optimization_barrier((encode(kspace, line_index), coil_maps))
    arrived = lax.all_to_all(
        sent.reshape(CX * SLABS, BLOCK // 4, 4, 128), ("cx", "slab"), split_axis=0, concat_axis=0, tiled=True
    ).reshape(SENT, 128)
    own, other = images(arrived, shared_maps(coil_maps))
    pairs = (own + from_partner(other, "core")).reshape(2, 4 * YL, NZ)
    far = lax.axis_index("zh")
    own = lax.dynamic_index_in_dim(pairs, far, 0, keepdims=False)
    other = lax.dynamic_index_in_dim(pairs, 1 - far, 0, keepdims=False)
    total = own + from_partner(other.astype(jnp.bfloat16), "zh").astype(jnp.float32)
    return jnp.transpose(total.reshape(2, YL, 2, NZ), (0, 2, 1, 3))


def solution(mesh):
    fine = Mesh(mesh.devices.reshape(CX, 2, 2, SLABS), ("cx", "zh", "core", "slab"))
    coil = ("cx", "zh", "core")
    placed = (
        P(None, coil, None, None, "slab", None),
        P(None, coil, None, "slab", None),
        P(None, "slab", None),
    )
    return jax.shard_map(
        local, mesh=fine, in_specs=placed, out_specs=P(coil, None, "slab", None), check_vma=False
    )
```

```python
import functools
import math

import jax
import jax.numpy as jnp
import numpy as np
from jax import lax
from jax.experimental import pallas as pl
from jax.experimental.pallas import tpu as pltpu
from jax.sharding import Mesh
from jax.sharding import PartitionSpec as P

NY = 384
NZ = 384
PHASES = 8
SLABS = 32
YL = NY // SLABS
KZL = NZ // SLABS
CX = 4
XL = 8
BLOCK = 3 * KZL
QUARTER = NY // 4
SENT = CX * SLABS * BLOCK
APART = CX * BLOCK
SPREAD = APART + 4
PADDED = (SLABS + 2) * SPREAD


def dft(rows, cols, length):
    turns = np.outer(rows, cols) % length
    angles = turns * (2.0 * math.pi / length)
    scaling = 1.0 / math.sqrt(length)
    return np.cos(angles) * scaling, np.sin(angles) * scaling


@functools.cache
def row_table():
    y = (np.arange(YL)[:, None] + np.arange(SLABS // 4)[None, :] * YL).reshape(-1)
    parts = [np.concatenate(dft(y, np.arange(residue, NY, 4), NY), axis=1) for residue in range(4)]
    return np.stack(parts).astype(jnp.bfloat16)


@functools.cache
def depth_table():
    kz = (np.arange(KZL)[:, None] + np.arange(SLABS)[None, :] * KZL).reshape(-1)
    cosine, sine = dft(kz, np.arange(NZ), NZ)
    from_real = np.concatenate([cosine, sine], axis=1)
    from_imag = np.concatenate([-sine, cosine], axis=1)
    return np.concatenate([from_real, from_imag], axis=0).astype(jnp.bfloat16)


def encode_kernel(k_ref, line_ref, w_ref, out_ref, scratch):
    theta = 2.0 * math.pi / PHASES
    cosine = math.cos(theta)
    sine = math.sin(theta)
    row = lax.broadcasted_iota(jnp.int32, (NY, 128), 0)
    ky = 4 * (row % QUARTER) + row // QUARTER
    lanes = lax.broadcasted_iota(jnp.int32, (1, 128), 1)

    def grid_of(kz):
        early_re, early_im, late_re, late_im = (
            jnp.concatenate([k_ref[part, c, t, kz] for c in range(2)], axis=0)
            for t in range(2)
            for part in range(2)
        )
        late_re = late_re.astype(jnp.float32)
        late_im = late_im.astype(jnp.float32)
        turned_re = (cosine * late_re + sine * late_im).astype(jnp.bfloat16)
        turned_im = (cosine * late_im - sine * late_re).astype(jnp.bfloat16)
        early = jnp.concatenate([early_re, early_im, -early_im, early_re], axis=0)
        late = jnp.concatenate([turned_re, turned_im, -turned_im, turned_re], axis=0)
        samples = jnp.concatenate([early, late], axis=1)
        chosen = jnp.concatenate(
            [jnp.where(ky == line_ref[kz, t : t + 1, :], 1.0, 0.0).astype(jnp.bfloat16) for t in range(2)],
            axis=1,
        )
        placed = lax.dot_general(
            chosen, samples, (((1,), (1,)), ((), ())), preferred_element_type=jnp.float32
        ).astype(jnp.bfloat16)
        return [
            jnp.concatenate([placed[at : at + QUARTER, :128], placed[at : at + QUARTER, 128:]], axis=0)
            for at in range(0, NY, QUARTER)
        ]

    def exchange(a, b, bit):
        upper = (lanes & bit) != 0
        return (
            jnp.where(upper, pltpu.roll(b, bit, 1), a),
            jnp.where(upper, b, pltpu.roll(a, 128 - bit, 1)),
        )

    sign = jnp.where(lanes < 64, -1.0, 1.0)

    ahead = grid_of(0), grid_of(1)
    for pair in range(KZL // 2):
        first, second = ahead
        if pair + 1 < KZL // 2:
            ahead = grid_of(2 * pair + 2), grid_of(2 * pair + 3)
        both = [
            jnp.dot(w_ref[residue], jnp.concatenate([first[residue], second[residue]], axis=1), preferred_element_type=jnp.float32)
            for residue in range(4)
        ]
        for half in range(2):
            kz = 2 * pair + half
            f0, f1, f2, f3 = (part[:, half * 128 : half * 128 + 128] for part in both)
            even, odd = f0 + f2, f1 + f3
            cross, turned = f0 - f2, sign * pltpu.roll(f1 - f3, 64, 1)
            quarters = (even + odd, cross + turned, even - odd, cross - turned)
            for side in range(2):
                for third in range(3):
                    tiles = []
                    for y in range(4 * third, 4 * third + 4):
                        near, far = (q[8 * y : 8 * y + 8] for q in quarters[2 * side : 2 * side + 2])
                        tiles.append(jnp.concatenate([near, far], axis=0).astype(jnp.bfloat16))
                    low = exchange(tiles[0], tiles[2], 16)
                    high = exchange(tiles[1], tiles[3], 16)
                    for upper in range(2):
                        for lower, value in enumerate(exchange(low[upper], high[upper], 8)):
                            start = (2 * upper + lower) * BLOCK + 16 * side * SPREAD + third * KZL + kz
                            scratch[pl.ds(start, 16, stride=SPREAD), :] = value.astype(jnp.float32)
    for slab in range(SLABS):
        out_ref[slab * APART : (slab + 1) * APART] = scratch[slab * SPREAD : slab * SPREAD + APART].astype(jnp.bfloat16)


def encode(kspace, line_index):
    return pl.pallas_call(
        encode_kernel,
        out_shape=jax.ShapeDtypeStruct((SENT, 128), jnp.bfloat16),
        in_specs=[pl.BlockSpec(memory_space=pltpu.VMEM)] * 3,
        out_specs=pl.BlockSpec(memory_space=pltpu.VMEM),
        scratch_shapes=[pltpu.VMEM((PADDED, 128), jnp.float32)],
        name="encode",
    )(jnp.transpose(kspace, (0, 1, 2, 4, 3, 5)), jnp.transpose(line_index, (1, 0, 2)), jnp.asarray(row_table()))


def image_kernel(me_ref, r_ref, m0_ref, m1_ref, m2_ref, m3_ref, d_ref, own_ref, other_ref, wide, lhs, sums):
    for slab in range(SLABS):
        wide[slab * SPREAD : slab * SPREAD + APART] = r_ref[slab * APART : (slab + 1) * APART].astype(jnp.float32)
    column = me_ref[0]
    core = me_ref[1]
    for third in range(3):
        for step in range(CX):
            base = (column ^ step) * BLOCK
            rows = jnp.concatenate(
                [wide[pl.ds(base + third * KZL + kz, SLABS, stride=SPREAD), :] for kz in range(KZL)], axis=0
            )
            turned = rows.T.astype(jnp.bfloat16)
            lhs[third, step * 64 : step * 64 + 64, : KZL * SLABS] = turned[:64]
            lhs[third, step * 64 : step * 64 + 64, KZL * SLABS :] = turned[64:]
        image = jnp.dot(lhs[third], d_ref[...], preferred_element_type=jnp.float32)
        real = imag = None
        for step, m_ref in enumerate((m0_ref, m1_ref, m2_ref, m3_ref)):
            for c in range(2):
                at = step * 64 + c * 32
                image_re = image[at : at + 32, :NZ]
                image_im = image[at : at + 32, NZ:]
                map_re, map_im = (
                    m_ref[part, c, 4 * third : 4 * third + 4].astype(jnp.float32).reshape(32, NZ) for part in range(2)
                )
                add_re = map_re * image_re + map_im * image_im
                add_im = map_re * image_im - map_im * image_re
                real, imag = (add_re, add_im) if real is None else (real + add_re, imag + add_im)
        for part, value in enumerate((real, imag)):
            for y in range(4):
                for lane in range(3):
                    sums[lane, pl.ds(2 * (4 * third + y) + part, XL, stride=2 * YL), :] = value[
                        y * 8 : y * 8 + 8, lane * 128 : lane * 128 + 128
                    ]
    rows = 4 * YL
    for zh in range(2):
        for lane in range(3):
            at = slice(lane * 128, lane * 128 + 128)
            own_ref[zh * rows : zh * rows + rows, at] = sums[lane, pl.ds((2 * zh + core) * rows, rows), :]
            other_ref[zh * rows : zh * rows + rows, at] = sums[lane, pl.ds((2 * zh + 1 - core) * rows, rows), :]


def images(arrived, maps):
    me = jnp.stack([lax.axis_index("cx"), lax.axis_index("core")]).astype(jnp.int32)
    vmem = pl.BlockSpec(memory_space=pltpu.VMEM)
    half = jax.ShapeDtypeStruct((8 * YL, NZ), jnp.float32)
    return pl.pallas_call(
        image_kernel,
        out_shape=(half, half),
        in_specs=[pl.BlockSpec(memory_space=pltpu.SMEM)] + [vmem] * 6,
        out_specs=(vmem, vmem),
        scratch_shapes=[
            pltpu.VMEM((PADDED, 128), jnp.float32),
            pltpu.VMEM((3, 4 * 64, 2 * NZ), jnp.bfloat16),
            pltpu.VMEM((3, 2 * YL * (XL + 1), 128), jnp.float32),
        ],
        compiler_params=pltpu.CompilerParams(vmem_limit_bytes=24 << 20),
        name="images",
    )(me, *(pltpu.with_memory_space_constraint(x, pltpu.VMEM) for x in (arrived, *maps, jnp.asarray(depth_table()))))


def shared_maps(coil_maps):
    rows = jnp.transpose(coil_maps, (0, 1, 3, 2, 4))
    column = lax.axis_index("cx")
    chunks = []
    for step in range(CX):
        chunk = lax.dynamic_slice_in_dim(rows, (column ^ step) * XL, XL, axis=3)
        if step:
            chunk = lax.ppermute(chunk, "cx", [(i, i ^ step) for i in range(CX)])
        chunks.append(chunk)
    return chunks


def from_partner(value, axis):
    pair = lax.all_gather(value, axis)
    return lax.dynamic_index_in_dim(pair, 1 - lax.axis_index(axis), 0, keepdims=False)


def local(kspace, coil_maps, line_index):
    sent, coil_maps = lax.optimization_barrier((encode(kspace, line_index), coil_maps))
    arrived = lax.all_to_all(
        sent.reshape(CX * SLABS, BLOCK // 4, 4, 128), ("slab", "cx"), split_axis=0, concat_axis=0, tiled=True
    ).reshape(SENT, 128)
    own, other = images(arrived, shared_maps(coil_maps))
    pairs = (own + from_partner(other, "core")).reshape(2, 4 * YL, NZ)
    far = lax.axis_index("zh")
    own = lax.dynamic_index_in_dim(pairs, far, 0, keepdims=False)
    other = lax.dynamic_index_in_dim(pairs, 1 - far, 0, keepdims=False)
    total = own + from_partner(other.astype(jnp.bfloat16), "zh").astype(jnp.float32)
    return jnp.transpose(total.reshape(2, YL, 2, NZ), (0, 2, 1, 3))


def solution(mesh):
    fine = Mesh(mesh.devices.reshape(CX, 2, 2, SLABS), ("cx", "zh", "core", "slab"))
    coil = ("cx", "zh", "core")
    placed = (
        P(None, coil, None, None, "slab", None),
        P(None, coil, None, "slab", None),
        P(None, "slab", None),
    )
    return jax.shard_map(
        local, mesh=fine, in_specs=placed, out_specs=P(coil, None, "slab", None), check_vma=False
    )
```
